512 devices in a mesh: blk: 32 (over x, y_hi, core), grp: 16 (over z, y_lo).
Axes of the slice: x: 4, y: 8 (y_hi: 4, y_lo: 2; y = y_hi * 2 + y_lo), z: 8, core: 2. Of those that a mesh axis runs over, the one named last changes fastest.
Arguments:
- amplitudes: bfloat16 [4096, 8, 4, 128], P('blk'), may hold values from -6 to 6
- integrals: bfloat16 [256, 4096, 128], P('grp', 'blk'), may hold values from -0.15625 to 0.15625
- virt_energy: float32 [4096], replicated, may hold values from 0.5 to 4
- pair_energy: float32 [8], replicated, may hold values from -3 to -0.5
- offsets: int32 [32, 4], replicated, may hold values from 0 to 31, as said below
Outputs:
- ladder: float32 [4096, 8, 4, 128], P(('blk', 'grp'))
- new_amplitudes: float32 [4096, 8, 4, 128], P(('blk', 'grp'))
The draws below stay inside these ranges and needn't reach their ends.
Inputs may be any that keep to these rules, and one draw needn't show every extreme that they name: The 4 offsets of one row tile are different; the first 3 are at most 2, the last is larger than 2.
All inputs are finite; a program needn't handle non-finite values.
Results may differ from the reference program's by a relative error of at most 0.0029.
Values may be sent and summed in bfloat16 or wider, within the bound.
No kernel may reach another device: no remote copies, remote signals or barrier semaphores. Data moves between devices by JAX's collectives and lax.ppermute only.
A program may use at most 64 MiB of HBM per device.

```python
import math
import jax
import jax.numpy as jnp
from jax import lax

VT = 128
NAUX = 256
NPAIR = 8
SLOTS = 4
DMAX = 2
NT = 32
NV = 4096


def draw_offsets(key, part):
    values = jnp.arange(DMAX + 1, dtype=jnp.int32)
    rows = jnp.arange(NT, dtype=jnp.int32)
    scores = jax.random.randint(key, (NT, DMAX + 1), 0, 1 << 20, dtype=jnp.int32) * (DMAX + 1) + values[None, :]
    forced = jax.random.randint(jax.random.fold_in(key, 7), (), 0, NT, dtype=jnp.int32)
    on_row = rows[:, None] == forced
    scores = jnp.where(on_row & (values[None, :] == 0), -1, scores)
    order = jnp.argsort(scores, axis=1, stable=True)[:, :SLOTS - 1]
    far_draw = jax.random.randint(jax.random.fold_in(key, 11), (NT,), DMAX + 1, NT, dtype=jnp.int32)
    far_draw = jnp.where(rows == forced, NT // 2, far_draw)
    far_draw = jnp.where(rows == (forced + 1) % NT, NT - 1, far_draw)
    return jnp.concatenate([order.astype(jnp.int32), far_draw[:, None].astype(jnp.int32)], axis=1)


def steps_of(stream_key, dims, shards, smallest, high):
    def one(position, shards_of):
        heights = jax.random.uniform(jax.random.fold_in(jax.random.fold_in(stream_key, 6), position), (shards_of,), jnp.float32, smallest / len(shards), high / len(shards))
        return jnp.repeat(jnp.exp(heights), dims[position] // shards_of).reshape((-1,) + (1,) * (len(dims) - position - 1))

    factor_of = one(*shards[0])
    for cut in shards[1:]:
        factor_of = factor_of * one(*cut)
    return factor_of


def gaussian(stream_key, shape, width, bound, shards=(), kind=jnp.bfloat16):
    result = width * jax.random.normal(stream_key, shape, jnp.float32)
    if shards:
        result = result * steps_of(stream_key, shape, shards, -0.22, 0.18)
    return jnp.clip(result, -bound, bound).astype(kind)


def setup_inputs(seed: int = 0) -> dict:
    key_list = jax.random.split(jax.random.key(seed), 6)
    amplitudes = gaussian(key_list[0], (NV, NPAIR, SLOTS, VT), 1.0, 6.0, ((0, 32),))
    integrals = gaussian(key_list[1], (NAUX, NV, VT), (VT * 11) ** -0.5, 0.15625, ((0, 16), (1, 32)))
    virt_energy = jnp.clip(jnp.exp(jax.random.uniform(key_list[2], (NV,), jnp.float32, math.log(0.5), math.log(4.0))), 0.5, 4.0)
    pair_energy = jnp.clip(jax.random.uniform(key_list[3], (NPAIR,), jnp.float32, -3.0, -0.5), -3.0, -0.5)
    offsets = draw_offsets(jax.random.fold_in(key_list[5], 71), 0)
    return {"amplitudes": amplitudes, "integrals": integrals, "virt_energy": virt_energy, "pair_energy": pair_energy, "offsets": offsets}


def reference(amplitudes, integrals, virt_energy, pair_energy, offsets):
    ntile = NV // VT
    amp = amplitudes.reshape(ntile, VT, NPAIR * SLOTS * VT)
    blocks = integrals.reshape(NAUX, ntile, VT, VT)
    rows = jnp.arange(ntile, dtype=jnp.int32)
    cols = ((rows[:, None] - offsets) % ntile).astype(jnp.int32)

    def one_tile(k):
        own = blocks[:, k]
        col_blocks = jnp.take(blocks, cols[k], axis=1)
        amp_tile = amp[k]

        def add_aux(total, q):
            half_split = jnp.dot(own[q], amp_tile, preferred_element_type=jnp.float32).astype(jnp.bfloat16)
            half_split = lax.optimization_barrier(half_split).astype(jnp.float32).reshape(VT, NPAIR, SLOTS, VT)
            term = jnp.einsum("apsd,sbd->apsb", half_split, col_blocks[q].astype(jnp.float32))
            return total + term, None

        start = jnp.zeros((VT, NPAIR, SLOTS, VT), jnp.float32)
        total, _ = lax.scan(add_aux, start, jnp.arange(NAUX, dtype=jnp.int32))
        return total

    ladder = lax.map(one_tile, rows)
    table = virt_energy.reshape(ntile, VT)
    col_energy = table[cols]
    denom = (table[:, :, None, None, None] + col_energy[:, None, None, :, :]
             - pair_energy[None, None, :, None, None])
    old = amplitudes.astype(jnp.float32).reshape(ntile, VT, NPAIR, SLOTS, VT)
    new_amplitudes = old - ladder / denom
    return (ladder.reshape(NV, NPAIR, SLOTS, VT), new_amplitudes.reshape(NV, NPAIR, SLOTS, VT))
```

```python
import functools

import jax
import jax.numpy as jnp
from jax import lax
from jax.experimental import pallas as pl
from jax.experimental.pallas import tpu as pltpu
from jax.sharding import PartitionSpec as P


QUAD = 4


def pick_kernel(index_ref, source_ref, out_ref, sem):
    def copy(row):
        return pltpu.make_async_copy(source_ref.at[index_ref[row]], out_ref.at[row], sem.at[row])

    rows = out_ref.shape[0]
    for row in range(rows):
        copy(row).start()
    for row in range(rows):
        copy(row).wait()


def pick_rows(source, index):
    return pl.pallas_call(
        pick_kernel,
        out_shape=jax.ShapeDtypeStruct(source.shape, source.dtype),
        in_specs=[
            pl.BlockSpec(memory_space=pltpu.SMEM),
            pl.BlockSpec(memory_space=pl.ANY),
        ],
        out_specs=pl.BlockSpec(memory_space=pltpu.VMEM),
        scratch_shapes=[pltpu.SemaphoreType.DMA((source.shape[0],))],
        cost_estimate=pl.CostEstimate(flops=0, transcendentals=0, bytes_accessed=4 * source.size),
        name="pick_rows",
    )(index, source)


def ladder_kernel(tiles, amps, rows_from, cols_from, job_ref, *refs):
    tile_refs, amp_refs = refs[:tiles], refs[tiles : tiles + amps]
    head_refs, (out_ref, *scratch) = refs[tiles + amps : -6], refs[-6:]
    own_ref, cols_ref, amp_ref, half_ref, total_ref = scratch
    aux, width = tile_refs[0].shape[0], tile_refs[0].shape[1]
    pairs, columns = half_ref.shape[0], total_ref.shape[0]
    head = sum(ref.shape[1] for ref in head_refs)
    jobs = (out_ref.shape[1] - head) // columns
    for ref in head_refs:
        out_ref[:, :head] = ref[...]

    @pl.loop(0, jobs)
    def _(job):
        for number in rows_from:

            @pl.when(job_ref[0, job] == number)
            def _():
                own_ref[...] = tile_refs[number][...]

        for number in cols_from:

            @pl.when(job_ref[1, job] == number)
            def _():
                for q in range(aux):
                    cols_ref[q // QUAD, :, (q % QUAD) * width : (q % QUAD + 1) * width] = tile_refs[
                        number
                    ][q]

        for number in range(amps):

            @pl.when(job_ref[2, job] == number)
            def _():
                amp_ref[...] = amp_refs[number][job_ref[3, job]]

        total_ref[...] = jnp.zeros_like(total_ref)

        @pl.loop(0, aux // QUAD)
        def _(step):
            rows = own_ref[pl.ds(step * QUAD, QUAD)].reshape(QUAD * width, width)
            for p in range(0, pairs, 2):
                half = jnp.dot(
                    rows,
                    amp_ref[:, p * width : (p + 2) * width],
                    preferred_element_type=jnp.float32,
                ).astype(jnp.bfloat16)
                for k in range(2):
                    for q in range(QUAD):
                        half_ref[p + k, :, q * width : (q + 1) * width] = half[
                            q * width : (q + 1) * width, k * width : (k + 1) * width
                        ]
            total_ref[...] += lax.dot_general(
                half_ref[...].reshape(pairs * width, QUAD * width),
                cols_ref[step],
                (((1,), (1,)), ((), ())),
                preferred_element_type=jnp.float32,
            )

        for p in range(pairs):
            start = pl.multiple_of(head + job * columns + p * width, width)
            out_ref[:, pl.ds(start, width)] = total_ref[p * width : (p + 1) * width, :].astype(
                jnp.bfloat16
            )


def partial_ladder(jobs, tiles, amps, heads, rows_from, cols_from):
    aux, width, _ = tiles[0].shape
    columns = amps[0].shape[2]
    pairs, count = columns // width, jobs.shape[1]
    arrays = [*tiles, *amps, *heads]
    total = sum(head.shape[1] for head in heads) + count * columns
    return pl.pallas_call(
        functools.partial(ladder_kernel, len(tiles), len(amps), rows_from, cols_from),
        out_shape=jax.ShapeDtypeStruct((width, total), jnp.bfloat16),
        in_specs=[pl.BlockSpec(memory_space=pltpu.SMEM)]
        + [pl.BlockSpec(memory_space=pltpu.VMEM)] * len(arrays),
        out_specs=pl.BlockSpec(memory_space=pltpu.VMEM),
        scratch_shapes=[
            pltpu.VMEM((aux, width, width), jnp.bfloat16),
            pltpu.VMEM((aux // QUAD, width, QUAD * width), jnp.bfloat16),
            pltpu.VMEM((width, columns), jnp.bfloat16),
            pltpu.VMEM((pairs, width, QUAD * width), jnp.bfloat16),
            pltpu.VMEM((columns, width), jnp.float32),
        ],
        cost_estimate=pl.CostEstimate(
            flops=4 * count * aux * width * width * columns,
            transcendentals=0,
            bytes_accessed=2 * sum(a.size for a in arrays) + 2 * width * total,
        ),
        compiler_params=pltpu.CompilerParams(vmem_limit_bytes=32 * 1024 * 1024),
    )(jobs, *arrays)


def local(amplitudes, integrals, virt_energy, pair_energy, offsets):
    tiles = lax.axis_size("blk")
    groups = lax.axis_size("grp")
    tile_index = lax.axis_index("blk")
    group_index = lax.axis_index("grp")
    aux, width, _ = integrals.shape
    pairs, slots = amplitudes.shape[1], amplitudes.shape[2]
    near = slots - 1
    rows = width // groups
    numbers = jnp.arange(tiles, dtype=jnp.int32)
    odd = tile_index % 2
    even_tiles, odd_tiles = range(0, tiles, 2), range(1, tiles, 2)

    own_offsets = lax.dynamic_slice_in_dim(offsets, tile_index, 1, 0)[0]
    slot_of = jnp.argmax(
        own_offsets[None, :near] == jnp.arange(near, dtype=jnp.int32)[:, None], axis=1
    ).astype(jnp.int32)

    spread = lax.all_to_all(
        integrals.reshape(tiles, aux * width // tiles, width), "blk", 0, 0, tiled=True
    )
    hop = [(i, (i + 2) % tiles) for i in odd_tiles] + [(i, (i - 2) % tiles) for i in even_tiles]
    across = lax.ppermute(integrals, "blk", hop)
    beside = lax.ppermute(integrals, "blk", [(i, i + 1) for i in even_tiles])
    amps = amplitudes.transpose(2, 0, 1, 3).reshape(slots, width, pairs * width)
    amps_above = lax.ppermute(
        lax.dynamic_slice_in_dim(amps, slot_of[2], 1, 0),
        "blk",
        [(i, (i - 2) % tiles) for i in even_tiles],
    )
    far_index = (numbers - offsets[:, near]) % tiles
    picked = pick_rows(spread, far_index)
    far = lax.all_to_all(picked, "blk", 0, 0, tiled=True).reshape(integrals.shape)
    before = lax.ppermute(across, "blk", [(i, i - 1) for i in odd_tiles])

    zero, one = jnp.int32(0), jnp.int32(1)

    jobs = jnp.stack([zero, zero, zero, slot_of[0]]).reshape(4, 1)
    piece = partial_ladder(jobs, [integrals], [amps], [], (0,), (0,))
    jobs = jnp.stack(
        [
            jnp.stack([zero, 1 - odd]),
            jnp.stack([3 - odd, odd]),
            jnp.stack([zero, 1 - odd]),
            jnp.stack([slot_of[1], odd * slot_of[2]]),
        ]
    ).astype(jnp.int32)
    piece = partial_ladder(
        jobs, [integrals, across, beside, before], [amps, amps_above], [piece], (0, 1), (0, 1, 2, 3)
    )
    jobs = jnp.stack([zero, one, zero, jnp.int32(near)]).reshape(4, 1)
    piece = partial_ladder(jobs, [integrals, far], [amps], [piece], (0,), (1,))
    sums = lax.all_to_all(piece.reshape(groups, rows, -1), "grp", 0, 0, tiled=True)
    sums = jnp.sum(sums.astype(jnp.float32), axis=0).reshape(rows, slots, pairs, width)
    near_sum, far_sum = sums[:, :near], sums[:, near]

    third = near_sum[:, 2]
    carried = lax.ppermute(third, "blk", [(i, (i + 2) % tiles) for i in even_tiles])
    third = jnp.where(odd == 1, third, carried)
    parts = [
        jnp.where(
            own_offsets[s] == 0, near_sum[:, 0], jnp.where(own_offsets[s] == 1, near_sum[:, 1], third)
        )
        for s in range(near)
    ]
    ladder = jnp.stack(parts + [far_sum], axis=2)

    first_row = group_index * rows
    old_rows = lax.dynamic_slice_in_dim(amplitudes, first_row, rows, 0).astype(jnp.float32)
    row_energy = lax.dynamic_slice_in_dim(virt_energy, tile_index * width + first_row, rows, 0)
    cols = (tile_index - own_offsets) % tiles
    table = virt_energy.reshape(tiles, width)
    chosen = cols[:, None, None] == numbers[None, :, None]
    col_energy = jnp.sum(jnp.where(chosen, table[None], 0.0), axis=1)
    denom = (
        row_energy[:, None, None, None]
        + col_energy[None, None, :, :]
        - pair_energy[None, :, None, None]
    )
    return (ladder, old_rows - ladder / denom)


def solution(mesh):
    placed = (P("blk", None, None, None), P("grp", "blk", None), P(), P(), P())
    return jax.shard_map(
        local,
        mesh=mesh,
        in_specs=placed,
        out_specs=(P(("blk", "grp"), None, None, None), P(("blk", "grp"), None, None, None)),
        check_vma=False,
    )
```

```python
import functools

import jax
import jax.numpy as jnp
from jax import lax
from jax.experimental import pallas as pl
from jax.experimental.pallas import tpu as pltpu
from jax.sharding import PartitionSpec as P


QUAD = 4


def pick_kernel(index_ref, source_ref, out_ref, sem):
    def copy(row):
        return pltpu.make_async_copy(source_ref.at[index_ref[row]], out_ref.at[row], sem.at[row])

    rows = out_ref.shape[0]
    for row in range(rows):
        copy(row).start()
    for row in range(rows):
        copy(row).wait()


def pick_rows(source, index):
    return pl.pallas_call(
        pick_kernel,
        out_shape=jax.ShapeDtypeStruct(source.shape, source.dtype),
        in_specs=[
            pl.BlockSpec(memory_space=pltpu.SMEM),
            pl.BlockSpec(memory_space=pl.ANY),
        ],
        out_specs=pl.BlockSpec(memory_space=pltpu.VMEM),
        scratch_shapes=[pltpu.SemaphoreType.DMA((source.shape[0],))],
        cost_estimate=pl.CostEstimate(flops=0, transcendentals=0, bytes_accessed=4 * source.size),
        name="pick_rows",
    )(index, source)


def ladder_kernel(tiles, amps, job, rows_from, cols_from, job_ref, *refs):
    tile_refs, amp_refs = refs[:tiles], refs[tiles : tiles + amps]
    head_refs, (out_ref, *scratch) = refs[tiles + amps : -6], refs[-6:]
    own_ref, cols_ref, amp_ref, half_ref, total_ref = scratch
    aux, width = tile_refs[0].shape[0], tile_refs[0].shape[1]
    pairs, columns = half_ref.shape[0], total_ref.shape[0]
    head = out_ref.shape[1] - columns
    for number, ref in enumerate(head_refs):
        place = min(number, head // columns - 1) * columns

        @pl.when(job_ref[job, 4] != number)
        def _():
            out_ref[:, place : place + columns] = ref[...]

    for number in rows_from:

        @pl.when(job_ref[job, 0] == number)
        def _():
            own_ref[...] = tile_refs[number][...]

    for number in cols_from:

        @pl.when(job_ref[job, 1] == number)
        def _():
            for q in range(aux):
                cols_ref[q // QUAD, :, (q % QUAD) * width : (q % QUAD + 1) * width] = tile_refs[
                    number
                ][q]

    for number in range(amps):

        @pl.when(job_ref[job, 2] == number)
        def _():
            amp_ref[...] = amp_refs[number][job_ref[job, 3]]

    total_ref[...] = jnp.zeros_like(total_ref)

    @pl.loop(0, aux // QUAD)
    def _(step):
        rows = own_ref[pl.ds(step * QUAD, QUAD)].reshape(QUAD * width, width)
        for p in range(0, pairs, 2):
            half = jnp.dot(
                rows,
                amp_ref[:, p * width : (p + 2) * width],
                preferred_element_type=jnp.float32,
            ).astype(jnp.bfloat16)
            for k in range(2):
                for q in range(QUAD):
                    half_ref[p + k, :, q * width : (q + 1) * width] = half[
                        q * width : (q + 1) * width, k * width : (k + 1) * width
                    ]
        total_ref[...] += lax.dot_general(
            half_ref[...].reshape(pairs * width, QUAD * width),
            cols_ref[step],
            (((1,), (1,)), ((), ())),
            preferred_element_type=jnp.float32,
        )

    for p in range(pairs):
        start = head + p * width
        out_ref[:, start : start + width] = total_ref[p * width : (p + 1) * width, :].astype(
            jnp.bfloat16
        )


def partial_ladder(jobs, job, tiles, amps, heads, rows_from, cols_from):
    aux, width, _ = tiles[0].shape
    columns = amps[0].shape[2]
    pairs = columns // width
    arrays = [*tiles, *amps, *heads]
    total = max(len(heads), 1) * columns
    return pl.pallas_call(
        functools.partial(ladder_kernel, len(tiles), len(amps), job, rows_from, cols_from),
        out_shape=jax.ShapeDtypeStruct((width, total), jnp.bfloat16),
        in_specs=[pl.BlockSpec(memory_space=pltpu.SMEM)]
        + [pl.BlockSpec(memory_space=pltpu.VMEM)] * len(arrays),
        out_specs=pl.BlockSpec(memory_space=pltpu.VMEM),
        scratch_shapes=[
            pltpu.VMEM((aux, width, width), jnp.bfloat16),
            pltpu.VMEM((aux // QUAD, width, QUAD * width), jnp.bfloat16),
            pltpu.VMEM((width, columns), jnp.bfloat16),
            pltpu.VMEM((pairs, width, QUAD * width), jnp.bfloat16),
            pltpu.VMEM((columns, width), jnp.float32),
        ],
        cost_estimate=pl.CostEstimate(
            flops=4 * aux * width * width * columns,
            transcendentals=0,
            bytes_accessed=2 * sum(a.size for a in arrays) + 2 * width * total,
        ),
        compiler_params=pltpu.CompilerParams(vmem_limit_bytes=32 * 1024 * 1024),
    )(jobs, *arrays)


def local(amplitudes, integrals, virt_energy, pair_energy, offsets):
    tiles = lax.axis_size("blk")
    groups = lax.axis_size("grp")
    tile_index = lax.axis_index("blk")
    group_index = lax.axis_index("grp")
    aux, width, _ = integrals.shape
    pairs, slots = amplitudes.shape[1], amplitudes.shape[2]
    near = slots - 1
    rows = width // groups
    numbers = jnp.arange(tiles, dtype=jnp.int32)
    odd = tile_index % 2
    even_tiles, odd_tiles = range(0, tiles, 2), range(1, tiles, 2)

    own_offsets = lax.dynamic_slice_in_dim(offsets, tile_index, 1, 0)[0]
    slot_of = jnp.argmax(
        own_offsets[None, :near] == jnp.arange(near, dtype=jnp.int32)[:, None], axis=1
    ).astype(jnp.int32)

    spread = lax.all_to_all(
        integrals.reshape(tiles, aux * width // tiles, width), "blk", 0, 0, tiled=True
    )
    hop = [(i, (i + 2) % tiles) for i in odd_tiles] + [(i, (i - 2) % tiles) for i in even_tiles]
    across = lax.ppermute(integrals, "blk", hop)
    beside = lax.ppermute(integrals, "blk", [(i, i + 1) for i in even_tiles])
    amps = amplitudes.transpose(2, 0, 1, 3).reshape(slots, width, pairs * width)
    amps_above = lax.ppermute(
        lax.dynamic_slice_in_dim(amps, slot_of[2], 1, 0),
        "blk",
        [(i, (i - 2) % tiles) for i in even_tiles],
    )
    far_index = (numbers - offsets[:, near]) % tiles
    picked = pick_rows(spread, far_index)
    far = lax.all_to_all(picked, "blk", 0, 0, tiled=True).reshape(integrals.shape)
    before = lax.ppermute(across, "blk", [(i, i - 1) for i in odd_tiles])

    entry, row = jnp.arange(5)[None, :], jnp.arange(4)[:, None]
    jobs = jnp.where(entry == 4, -1, 0)
    for at, value in (
        ((0, 3), slot_of[0]),
        ((1, 0), 1 - odd),
        ((1, 1), odd),
        ((1, 2), 1 - odd),
        ((1, 3), odd * slot_of[2]),
        ((2, 1), 2 - odd),
        ((2, 3), slot_of[1]),
        ((3, 1), 1),
        ((3, 3), near),
        ((3, 4), 3 - odd),
    ):
        jobs = jnp.where((row == at[0]) & (entry == at[1]), value, jobs)
    jobs = jobs.astype(jnp.int32)

    same = partial_ladder(jobs, 0, [integrals], [amps], [], (0,), (0,))
    cross = partial_ladder(jobs, 1, [integrals, across], [amps, amps_above], [], (0, 1), (0, 1))
    handed = lax.ppermute(cross, "blk", [(i, (i + 2) % tiles) for i in even_tiles])
    following = partial_ladder(jobs, 2, [integrals, beside, before], [amps], [], (0,), (1, 2))
    piece = partial_ladder(
        jobs, 3, [integrals, far], [amps], [same, following, handed, cross], (0,), (1,)
    )
    sums = lax.all_to_all(piece.reshape(groups, rows, -1), "grp", 0, 0, tiled=True)
    sums = jnp.sum(sums.astype(jnp.float32), axis=0).reshape(rows, slots, pairs, width)
    near_sum, far_sum = sums[:, :near], sums[:, near]

    parts = [
        jnp.where(
            own_offsets[s] == 0, near_sum[:, 0], jnp.where(own_offsets[s] == 1, near_sum[:, 1], near_sum[:, 2])
        )
        for s in range(near)
    ]
    ladder = jnp.stack(parts + [far_sum], axis=2)

    first_row = group_index * rows
    old_rows = lax.dynamic_slice_in_dim(amplitudes, first_row, rows, 0).astype(jnp.float32)
    row_energy = lax.dynamic_slice_in_dim(virt_energy, tile_index * width + first_row, rows, 0)
    cols = (tile_index - own_offsets) % tiles
    table = virt_energy.reshape(tiles, width)
    chosen = cols[:, None, None] == numbers[None, :, None]
    col_energy = jnp.sum(jnp.where(chosen, table[None], 0.0), axis=1)
    denom = (
        row_energy[:, None, None, None]
        + col_energy[None, None, :, :]
        - pair_energy[None, :, None, None]
    )
    return (ladder, old_rows - ladder / denom)


def solution(mesh):
    placed = (P("blk", None, None, None), P("grp", "blk", None), P(), P(), P())
    return jax.shard_map(
        local,
        mesh=mesh,
        in_specs=placed,
        out_specs=(P(("blk", "grp"), None, None, None), P(("blk", "grp"), None, None, None)),
        check_vma=False,
    )
```

```python
import functools

import jax
import jax.numpy as jnp
from jax import lax
from jax.experimental import pallas as pl
from jax.experimental.pallas import tpu as pltpu
from jax.sharding import PartitionSpec as P


QUAD = 4
JOBS = (0, 0, 0, 0, -1, 1, 0, 1, 0, -1, 0, 2, 0, 0, -1, 0, 1, 0, 3, 3)
PARITY = (0, 0, 0, 0, 0, -1, 1, -1, 0, 0, 0, -1, 0, 0, 0, 0, 0, 0, 0, -1)
SLOT = (-1, -1, -1, 0, -1, -1, -1, -1, 2, -1, -1, -1, -1, 1, -1, -1, -1, -1, -1, -1)


def pick_kernel(index_ref, source_ref, out_ref):
    for row in range(out_ref.shape[0]):
        out_ref[row] = source_ref[index_ref[row]]


def pick_rows(source, index):
    return pl.pallas_call(
        pick_kernel,
        out_shape=jax.ShapeDtypeStruct(source.shape, source.dtype),
        in_specs=[
            pl.BlockSpec(memory_space=pltpu.SMEM),
            pl.BlockSpec(memory_space=pltpu.VMEM),
        ],
        out_specs=pl.BlockSpec(memory_space=pltpu.VMEM),
        cost_estimate=pl.CostEstimate(flops=0, transcendentals=0, bytes_accessed=4 * source.size),
        name="pick_rows",
    )(index, source)


def ladder_kernel(tiles, amps, job, rows_from, cols_from, job_ref, *refs):
    tile_refs, amp_refs = refs[:tiles], refs[tiles : tiles + amps]
    head_refs, (out_ref, *scratch) = refs[tiles + amps : -6], refs[-6:]
    own_ref, cols_ref, amp_ref, half_ref, total_ref = scratch
    aux, width = tile_refs[0].shape[0], tile_refs[0].shape[1]
    pairs, columns = half_ref.shape[0], total_ref.shape[0]
    head = out_ref.shape[1] - columns
    for number, ref in enumerate(head_refs):
        place = min(number, head // columns - 1) * columns

        @pl.when(job_ref[job, 4] != number)
        def _():
            out_ref[:, place : place + columns] = ref[...]

    for number in rows_from:

        @pl.when(job_ref[job, 0] == number)
        def _():
            own_ref[...] = tile_refs[number][...]

    for number in cols_from:

        @pl.when(job_ref[job, 1] == number)
        def _():
            for q in range(aux):
                cols_ref[q // QUAD, :, (q % QUAD) * width : (q % QUAD + 1) * width] = tile_refs[
                    number
                ][q]

    for number in range(amps):

        @pl.when(job_ref[job, 2] == number)
        def _():
            amp_ref[...] = amp_refs[number][job_ref[job, 3]]

    total_ref[...] = jnp.zeros_like(total_ref)

    @pl.loop(0, aux // QUAD)
    def _(step):
        rows = own_ref[pl.ds(step * QUAD, QUAD)].reshape(QUAD * width, width)
        for p in range(0, pairs, 2):
            half = jnp.dot(
                rows,
                amp_ref[:, p * width : (p + 2) * width],
                preferred_element_type=jnp.float32,
            ).astype(jnp.bfloat16)
            for k in range(2):
                for q in range(QUAD):
                    half_ref[p + k, :, q * width : (q + 1) * width] = half[
                        q * width : (q + 1) * width, k * width : (k + 1) * width
                    ]
        total_ref[...] += lax.dot_general(
            half_ref[...].reshape(pairs * width, QUAD * width),
            cols_ref[step],
            (((1,), (1,)), ((), ())),
            preferred_element_type=jnp.float32,
        )

    for p in range(pairs):
        start = head + p * width
        out_ref[:, start : start + width] = total_ref[p * width : (p + 1) * width, :].astype(
            jnp.bfloat16
        )


def partial_ladder(jobs, job, tiles, amps, heads, rows_from, cols_from):
    aux, width, _ = tiles[0].shape
    columns = amps[0].shape[2]
    pairs = columns // width
    arrays = [*tiles, *amps, *heads]
    total = max(len(heads), 1) * columns
    return pl.pallas_call(
        functools.partial(ladder_kernel, len(tiles), len(amps), job, rows_from, cols_from),
        out_shape=jax.ShapeDtypeStruct((width, total), jnp.bfloat16),
        in_specs=[pl.BlockSpec(memory_space=pltpu.SMEM)]
        + [pl.BlockSpec(memory_space=pltpu.VMEM)] * len(arrays),
        out_specs=pl.BlockSpec(memory_space=pltpu.VMEM),
        scratch_shapes=[
            pltpu.VMEM((aux, width, width), jnp.bfloat16),
            pltpu.VMEM((aux // QUAD, width, QUAD * width), jnp.bfloat16),
            pltpu.VMEM((width, columns), jnp.bfloat16),
            pltpu.VMEM((pairs, width, QUAD * width), jnp.bfloat16),
            pltpu.VMEM((columns, width), jnp.float32),
        ],
        cost_estimate=pl.CostEstimate(
            flops=4 * aux * width * width * columns,
            transcendentals=0,
            bytes_accessed=2 * sum(a.size for a in arrays) + 2 * width * total,
        ),
        compiler_params=pltpu.CompilerParams(vmem_limit_bytes=32 * 1024 * 1024),
    )(jobs, *arrays)


def local(amplitudes, integrals, virt_energy, pair_energy, offsets):
    tiles = lax.axis_size("blk")
    groups = lax.axis_size("grp")
    tile_index = lax.axis_index("blk")
    group_index = lax.axis_index("grp")
    aux, width, _ = integrals.shape
    pairs, slots = amplitudes.shape[1], amplitudes.shape[2]
    near = slots - 1
    rows = width // groups
    numbers = jnp.arange(tiles, dtype=jnp.int32)
    odd = tile_index % 2
    even_tiles, odd_tiles = range(0, tiles, 2), range(1, tiles, 2)

    own_offsets = lax.dynamic_slice_in_dim(offsets, tile_index, 1, 0)[0]
    slot_of = jnp.argmax(
        own_offsets[None, :near] == jnp.arange(near, dtype=jnp.int32)[:, None], axis=1
    ).astype(jnp.int32)

    spread = lax.all_to_all(
        integrals.reshape(tiles, aux * width // tiles, width), "blk", 0, 0, tiled=True
    )
    hop = [(i, (i + 2) % tiles) for i in odd_tiles] + [(i, (i - 2) % tiles) for i in even_tiles]
    across = lax.ppermute(integrals, "blk", hop)
    beside = lax.ppermute(integrals, "blk", [(i, i + 1) for i in even_tiles])
    amps = amplitudes.transpose(2, 0, 1, 3).reshape(slots, width, pairs * width)
    amps_above = lax.ppermute(
        lax.dynamic_slice_in_dim(amps, slot_of[2], 1, 0),
        "blk",
        [(i, (i - 2) % tiles) for i in even_tiles],
    )
    far_index = (numbers - offsets[:, near]) % tiles
    picked = pick_rows(spread, far_index)
    far = lax.all_to_all(picked, "blk", 0, 0, tiled=True).reshape(integrals.shape)
    before = lax.ppermute(across, "blk", [(i, i - 1) for i in odd_tiles])

    base = jnp.array(JOBS, jnp.int32).reshape(4, 5)
    flags = jnp.array(PARITY, jnp.int32).reshape(4, 5)
    slot = jnp.array(SLOT, jnp.int32).reshape(4, 5)
    jobs = base + flags * odd
    for number in range(near):
        jobs = jobs + jnp.where(
            (slot == number) & ((number < near - 1) | (odd == 1)), slot_of[number], 0
        )
    jobs = jobs.astype(jnp.int32)

    same = partial_ladder(jobs, 0, [integrals], [amps], [], (0,), (0,))
    cross = partial_ladder(jobs, 1, [integrals, across], [amps, amps_above], [], (0, 1), (0, 1))
    handed = lax.ppermute(cross, "blk", [(i, (i + 2) % tiles) for i in even_tiles])
    following = partial_ladder(jobs, 2, [integrals, beside, before], [amps], [], (0,), (1, 2))
    piece = partial_ladder(
        jobs, 3, [integrals, far], [amps], [same, following, handed, cross], (0,), (1,)
    )
    sums = lax.all_to_all(piece.reshape(groups, rows, -1), "grp", 0, 0, tiled=True)
    sums = jnp.sum(sums.astype(jnp.float32), axis=0).reshape(rows, slots, pairs, width)
    near_sum, far_sum = sums[:, :near], sums[:, near]

    parts = [
        jnp.where(
            own_offsets[s] == 0, near_sum[:, 0], jnp.where(own_offsets[s] == 1, near_sum[:, 1], near_sum[:, 2])
        )
        for s in range(near)
    ]
    ladder = jnp.stack(parts + [far_sum], axis=2)

    first_row = group_index * rows
    old_rows = lax.dynamic_slice_in_dim(amplitudes, first_row, rows, 0).astype(jnp.float32)
    row_energy = lax.dynamic_slice_in_dim(virt_energy, tile_index * width + first_row, rows, 0)
    cols = (tile_index - own_offsets) % tiles
    table = virt_energy.reshape(tiles, width)
    chosen = cols[:, None, None] == numbers[None, :, None]
    col_energy = jnp.sum(jnp.where(chosen, table[None], 0.0), axis=1)
    denom = (
        row_energy[:, None, None, None]
        + col_energy[None, None, :, :]
        - pair_energy[None, :, None, None]
    )
    return (ladder, old_rows - ladder / denom)


def solution(mesh):
    placed = (P("blk", None, None, None), P("grp", "blk", None), P(), P(), P())
    return jax.shard_map(
        local,
        mesh=mesh,
        in_specs=placed,
        out_specs=(P(("blk", "grp"), None, None, None), P(("blk", "grp"), None, None, None)),
        check_vma=False,
    )
```
